32 devices in a mesh: wide: 8 (over z, x), narrow: 4 (over y, core).
Axes of the slice: x: 2, y: 2, z: 4, core: 2. Of those that a mesh axis runs over, the one named last changes fastest.
Arguments:
- states: bfloat16 [32, 128, 1472], P(('wide', 'narrow')), may hold values from -6 to 6
- segment_ids: int32 [32, 128], P(('wide', 'narrow')), may hold values from 0 to 11, never falling along the last dimension, each value on 1 to 64 neighbouring positions
- attn_gain: bfloat16 [1472], P('wide'), may hold values from 0.5 to 1.5
- w_query: bfloat16 [1472, 384], P('wide', 'narrow'), may hold values from -0.0390625 to 0.0390625
- w_key: bfloat16 [1472, 384], P('wide', 'narrow'), may hold values from -0.15625 to 0.15625
- w_value: bfloat16 [1472, 384], P('wide', 'narrow'), may hold values from -0.15625 to 0.15625
- w_attn_out: bfloat16 [384, 1472], P('narrow', 'wide'), may hold values from -0.625 to 0.625
- bias_table: bfloat16 [32, 6], replicated, may hold values from -3 to 3
- mlp_gain: bfloat16 [1472], P('wide'), may hold values from 0.5 to 1.5
- w_in_gate: bfloat16 [1472, 3584], P('wide', 'narrow'), may hold values from -0.15625 to 0.15625
- w_in_up: bfloat16 [1472, 3584], P('wide', 'narrow'), may hold values from -0.15625 to 0.15625
- w_mlp_out: bfloat16 [3584, 1472], P('narrow', 'wide'), may hold values from -0.1875 to 0.1875
- gate_gain: bfloat16 [1472], P('wide'), may hold values from 0.5 to 1.5
- gate_weight: bfloat16 [1472], P('wide'), may hold values from -0.15625 to 0.15625
- out_cot: bfloat16 [32, 128, 1472], P(('wide', 'narrow')), may hold values from -6 to 6
- gate_cot: float32 [32, 128], P(('wide', 'narrow')), may hold values from -0.6 to 0.6
Outputs:
- out_states: bfloat16 [32, 128, 1472], P(('wide', 'narrow'))
- gate_values: float32 [32, 128], P(('wide', 'narrow'))
- grad_states: bfloat16 [32, 128, 1472], P(('wide', 'narrow'))
- grad_attn_gain: float32 [1472], P('wide')
- grad_query: float32 [1472, 384], P('wide', 'narrow')
- grad_key: float32 [1472, 384], P('wide', 'narrow')
- grad_value: float32 [1472, 384], P('wide', 'narrow')
- grad_attn_out: float32 [384, 1472], P('narrow', 'wide')
- grad_bias_table: float32 [32, 6], replicated
- grad_mlp_gain: float32 [1472], P('wide')
- grad_in_gate: float32 [1472, 3584], P('wide', 'narrow')
- grad_in_up: float32 [1472, 3584], P('wide', 'narrow')
- grad_mlp_out: float32 [3584, 1472], P('narrow', 'wide')
- grad_gate_gain: float32 [1472], P('wide')
- grad_gate_weight: float32 [1472], P('wide')
The draws below stay inside these ranges and needn't reach their ends.
Inputs may be any that keep to these rules, and one draw needn't show every extreme that they name: `segment_ids`: within each row the numbers never fall; each of 0 to 11 names a document of 1 to 64 tokens, and some document has exactly 64.
All inputs are finite; a program needn't handle non-finite values.
Results may differ from the reference program's by a relative error of at most 0.017.
Values may be sent and summed in bfloat16 or wider, within the bound.
No kernel may reach another device: no remote copies, remote signals or barrier semaphores. Data moves between devices by JAX's collectives and lax.ppermute only.
A program may use at most 256 MiB of HBM per device.

```python
import math
import jax
import jax.numpy as jnp
import numpy as np
from jax import lax

D = 1472
HEADS = 6
FF = 3584
BUCKETS = 32
LEN = 128
SEGS = 12
INNER = 384
ROWS = 32


def block_scale(rng, extent, shards, least, top_value):
    level = 1.0
    for position, shards_of in shards:
        heights = jax.random.uniform(jax.random.fold_in(jax.random.fold_in(rng, 6), position), (shards_of,), jnp.float32, least / len(shards), top_value / len(shards))
        level = level * jnp.repeat(jnp.exp(heights), extent[position] // shards_of).reshape((-1,) + (1,) * (len(extent) - 1 - position))
    return level


def split_up(amount, total, bound, skew):
    loads = [(1 << 20) // math.isqrt(grade ** skew) + 1 for grade in range(2, amount + 1)]
    surplus, counts = total - bound - (amount - 1), [1] * (amount - 1)
    while surplus > 0:
        free = [i for i in range(amount - 1) if counts[i] < bound]
        mass, budget = sum([loads[i] for i in free]), surplus
        for i in free:
            extra = min(bound - counts[i], max(1, budget * loads[i] // mass), surplus)
            counts[i] = counts[i] + extra
            surplus = surplus - extra
    return np.array([bound] + counts)


def uneven_parts(stream_key, number_of, total, most, skew):
    if number_of == 2:
        one = jax.random.randint(stream_key, (), max(1, total - most), min(most, total - 1) + 1)
        return jnp.stack([one, total - one])
    lengths = jnp.asarray(split_up(number_of, total, most, skew), jnp.int32)
    couples = (number_of - 1) // 2
    donor, taker = lengths[1:1 + 2 * couples:2], lengths[2:2 + 2 * couples:2]
    room = jnp.minimum(donor - 1, most - taker)
    passed = jax.random.randint(jax.random.fold_in(stream_key, 1), (couples,), 0, 1 << 20) % (room + 1)
    lengths = lengths.at[1:1 + 2 * couples:2].set(donor - passed).at[2:2 + 2 * couples:2].set(taker + passed)
    return lengths[jax.random.permutation(jax.random.fold_in(stream_key, 2), number_of)]


def centred(stream_key, shape, spread, most, pieces=(), kind=jnp.bfloat16):
    entries = jax.random.normal(stream_key, shape, jnp.float32) * spread
    if len(pieces) > 0:
        entries = block_scale(stream_key, shape, pieces, -0.22, 0.18) * entries
    return jnp.clip(entries, min=-most, max=most).astype(kind)


def setup_inputs(seed: int = 0) -> dict:
    key_of = jax.random.split(jax.random.key(seed), 17)
    states = centred(key_of[0], (ROWS, LEN, D), 1.0, 6.0, ((0, 32),))
    segment_ids = jax.vmap(lambda own: jnp.searchsorted(jnp.cumsum(uneven_parts(own, SEGS, LEN, LEN // 2, 2)), jnp.arange(LEN), side="right"))(jax.random.split(key_of[1], ROWS)).reshape((ROWS, LEN)).astype(jnp.int32)
    attn_gain = jnp.clip(1.0 + 0.1 * jax.random.normal(key_of[2], (D,), jnp.float32), 0.5, 1.5).astype(jnp.bfloat16)
    w_query = centred(key_of[3], (D, INNER), (16 * D) ** -0.5, 0.0390625, ((0, 8), (1, 4)))
    w_key = centred(key_of[4], (D, INNER), D ** -0.5, 0.15625, ((0, 8), (1, 4)))
    w_value = centred(key_of[5], (D, INNER), D ** -0.5, 0.15625, ((0, 8), (1, 4)))
    w_attn_out = centred(key_of[6], (INNER, D), (INNER // 4) ** -0.5, 0.625, ((0, 4), (1, 8)))
    bias_table = centred(key_of[7], (BUCKETS, HEADS), 0.5, 3.0)
    mlp_gain = jnp.clip(1.0 + 0.1 * jax.random.normal(key_of[8], (D,), jnp.float32), 0.5, 1.5).astype(jnp.bfloat16)
    w_in_gate = centred(key_of[9], (D, FF), D ** -0.5, 0.15625, ((0, 8), (1, 4)))
    w_in_up = centred(key_of[10], (D, FF), D ** -0.5, 0.15625, ((0, 8), (1, 4)))
    w_mlp_out = centred(key_of[11], (FF, D), (FF // 4) ** -0.5, 0.1875, ((0, 4), (1, 8)))
    gate_gain = jnp.clip(1.0 + 0.1 * jax.random.normal(key_of[12], (D,), jnp.float32), 0.5, 1.5).astype(jnp.bfloat16)
    gate_weight = centred(key_of[13], (D,), D ** -0.5, 0.15625, ((0, 8),))
    out_cot = centred(key_of[14], (ROWS, LEN, D), 1.0, 6.0, ((0, 32),))
    gate_cot = centred(key_of[15], (ROWS, LEN), 0.1, 0.6, ((0, 32),), jnp.float32)
    return dict(states=states, segment_ids=segment_ids, attn_gain=attn_gain, w_query=w_query, w_key=w_key, w_value=w_value, w_attn_out=w_attn_out, bias_table=bias_table, mlp_gain=mlp_gain, w_in_gate=w_in_gate, w_in_up=w_in_up, w_mlp_out=w_mlp_out, gate_gain=gate_gain, gate_weight=gate_weight, out_cot=out_cot, gate_cot=gate_cot)


EPS = 1e-06
NEGATIVE = -1000000000.0
LIMITS = (12, 16, 23, 32, 46, 64, 91)

@jax.custom_vjp
def low(v):
    return lax.optimization_barrier(v.astype(jnp.bfloat16)).astype(jnp.float32)

@jax.custom_vjp
def low_back(v):
    return v

def low_keep(v):
    return (low(v), None)

def low_pass(kept, grad):
    return (grad,)

def back_keep(v):
    return (v, None)

def back_low(kept, grad):
    return (low(grad),)
low.defvjp(low_keep, low_pass)
low_back.defvjp(back_keep, back_low)

def normalize(values, gain):
    scale = lax.rsqrt(lax.optimization_barrier(jnp.mean(values * values, axis=-1, keepdims=True)) + EPS)
    return values * scale * gain

def gelu_mix(gate_part, up_part):
    return jax.nn.gelu(gate_part, approximate=True) * up_part

def relative_buckets(length):
    offsets = jnp.arange(length, dtype=jnp.int32)
    rel = offsets[None, :] - offsets[:, None]
    dist = jnp.abs(rel)
    large = jnp.full(rel.shape, 8, jnp.int32)
    for limit in LIMITS:
        large = large + (dist >= limit).astype(jnp.int32)
    upper = jnp.where(rel > 0, jnp.int32(16), jnp.int32(0))
    return upper + jnp.where(dist < 8, dist, large)

def matmul(left, right):
    return jnp.einsum('rtd,de->rte', left, right, precision=lax.Precision.HIGHEST)

def forward(params, inputs, segments):
    attn_gain, w_query, w_key, w_value, w_attn_out, bias_table, mlp_gain, w_in_gate, w_in_up, w_mlp_out, gate_gain, gate_weight = params
    rows, length, width = inputs.shape
    heads = bias_table.shape[1]
    h1 = low(normalize(inputs, attn_gain))
    query = low(low_back(matmul(h1, w_query))).reshape(rows, length, heads, -1)
    key = low(low_back(matmul(h1, w_key))).reshape(rows, length, heads, -1)
    value = low(low_back(matmul(h1, w_value))).reshape(rows, length, heads, -1)
    buckets = relative_buckets(length)
    bias = jnp.transpose(jnp.take(bias_table, buckets, axis=0), (2, 0, 1))
    scores = jnp.einsum('rqhd,rkhd->rhqk', query, key, precision=lax.Precision.HIGHEST) + bias[None]
    scores = low_back(scores)
    same = segments[:, :, None] == segments[:, None, :]
    scores = jnp.where(same[:, None], scores, NEGATIVE)
    probs = low(jax.nn.softmax(scores, axis=-1))
    attended = jnp.einsum('rhqk,rkhd->rqhd', probs, value, precision=lax.Precision.HIGHEST)
    attended = low(low_back(attended)).reshape(rows, length, -1)
    x2 = inputs + low_back(matmul(attended, w_attn_out))
    h2 = low(normalize(x2, mlp_gain))
    gate_part = low_back(matmul(h2, w_in_gate))
    up_part = low_back(matmul(h2, w_in_up))
    act = low(gelu_mix(gate_part, up_part))
    x3 = x2 + low_back(matmul(act, w_mlp_out))
    h3 = normalize(x3, gate_gain)
    logits = lax.optimization_barrier(jnp.sum(h3 * gate_weight, axis=-1))
    return (x3, -30.0 * jax.nn.sigmoid(logits))

def reference(states, segment_ids, attn_gain, w_query, w_key, w_value, w_attn_out, bias_table, mlp_gain, w_in_gate, w_in_up, w_mlp_out, gate_gain, gate_weight, out_cot, gate_cot):
    params = tuple((a.astype(jnp.float32) for a in (attn_gain, w_query, w_key, w_value, w_attn_out, bias_table, mlp_gain, w_in_gate, w_in_up, w_mlp_out, gate_gain, gate_weight)))
    rows_span = max(1, min(ROWS, 4096 // LEN))
    steps_count = ROWS // rows_span
    inputs = states.astype(jnp.float32).reshape(steps_count, rows_span, LEN, D)
    segs = segment_ids.reshape(steps_count, rows_span, LEN)
    out_grads = out_cot.astype(jnp.float32).reshape(steps_count, rows_span, LEN, D)
    gate_grads = gate_cot.astype(jnp.float32).reshape(steps_count, rows_span, LEN)

    def step(totals, item):
        block, seg, out_grad, gate_grad = item
        outcome, pullback = jax.vjp(lambda p, x: forward(p, x, seg), params, block)
        param_grads, input_grad = pullback((out_grad, gate_grad))
        totals = jax.tree.map(lambda a, b: a + b, totals, param_grads)
        return (totals, (outcome[0].astype(jnp.bfloat16), outcome[1], input_grad.astype(jnp.bfloat16)))
    start = jax.tree.map(jnp.zeros_like, params)
    totals, (outputs, gates, input_grads) = lax.scan(step, start, (inputs, segs, out_grads, gate_grads))
    return (outputs.reshape(ROWS, LEN, D), gates.reshape(ROWS, LEN), input_grads.reshape(ROWS, LEN, D), totals[0], totals[1], totals[2], totals[3], totals[4], totals[5], totals[6], totals[7], totals[8], totals[9], totals[10], totals[11])
```

```python
import jax
import jax.numpy as jnp
from jax import lax
from jax.sharding import PartitionSpec as P

EPS = 1e-06
NEGATIVE = -1000000000.0
LIMITS = (12, 16, 23, 32, 46, 64, 91)
F32 = jnp.float32
BF16 = jnp.bfloat16


def inverse_rms(values):
    return lax.rsqrt(jnp.mean(values * values, axis=-1, keepdims=True) + EPS)


def norm_back(values, gain, grad):
    scale = inverse_rms(values)
    unit = values * scale
    inner = grad * gain
    back = scale * (inner - unit * jnp.mean(inner * unit, axis=-1, keepdims=True))
    return back, jnp.sum(grad * unit, axis=0)


def gelu_mix(gate_part, up_part):
    return jax.nn.gelu(gate_part, approximate=True) * up_part


def relative_buckets(length):
    offsets = jnp.arange(length, dtype=jnp.int32)
    rel = offsets[None, :] - offsets[:, None]
    dist = jnp.abs(rel)
    large = jnp.full(rel.shape, 8, jnp.int32)
    for limit in LIMITS:
        large = large + (dist >= limit).astype(jnp.int32)
    upper = jnp.where(rel > 0, jnp.int32(16), jnp.int32(0))
    return upper + jnp.where(dist < 8, dist, large)


def product(left, right):
    return jnp.dot(left, right, preferred_element_type=F32)


def times_back(left, right):
    return lax.dot_general(left, right, (((1,), (1,)), ((), ())), preferred_element_type=F32)


def outer_sum(left, right):
    return lax.dot_general(left, right, (((0,), (0,)), ((), ())), preferred_element_type=F32)


def swap(value, axis, step):
    count = lax.axis_size(axis)
    return lax.ppermute(value, axis, [(i, i ^ step) for i in range(count)])


def total_sum(value, axis):
    step = 1
    while step < lax.axis_size(axis):
        value = value + swap(value, axis, step)
        step *= 2
    return value


def gather_rows(rows):
    parts = [rows]
    step = lax.axis_size("narrow") // 2
    held = {0: rows}
    while step:
        held.update({k ^ step: swap(v, "narrow", step) for k, v in list(held.items())})
        step //= 2
    parts = [held[k] for k in range(lax.axis_size("narrow"))]
    return jnp.concatenate(parts, axis=0)


def scatter_rows(partial):
    count = lax.axis_size("narrow")
    length = partial.shape[0] // count
    held = {k: partial[k * length : (k + 1) * length] for k in range(count)}
    step = 1
    while step < count:
        kept = {}
        for k in held:
            if not k & step:
                there = swap(held[k ^ step].astype(BF16), "narrow", step)
                kept[k] = held[k].astype(F32) + there.astype(F32)
        held = kept
        step *= 2
    return held[0]


def to_features(parts):
    count = lax.axis_size("narrow")
    me = lax.axis_index("narrow")
    out = jnp.zeros((count,) + parts[0].shape, parts[0].dtype)
    for k in range(count):
        got = parts[k] if k == 0 else swap(parts[k], "narrow", k)
        out = lax.dynamic_update_slice(out, got[None], (me ^ k, 0, 0))
    return out


def to_rows(features):
    count = lax.axis_size("narrow")
    me = lax.axis_index("narrow")
    parts = []
    for k in range(count):
        piece = lax.dynamic_index_in_dim(features, me ^ k, 0, keepdims=False)
        parts.append(piece if k == 0 else swap(piece, "narrow", k))
    return jnp.concatenate(parts, axis=0)


def ring(value):
    count = lax.axis_size("wide")
    return lax.ppermute(value, "wide", [(w, (w + 2) % count) for w in range(count)])


def stepwise():
    return lax.axis_size("wide") == 8


def gather_blocks(block):
    if not stepwise():
        return lax.all_gather(block, "wide", axis=0)
    count = lax.axis_size("wide")
    lines = count // 2
    me = lax.axis_index("wide")
    line, side = me // 2, me % 2
    out = jnp.zeros((count,) + block.shape, block.dtype)
    held = block
    for k in range(lines):
        there = (line - k) % lines
        follow = ring(held) if k + 1 < lines else None
        other = swap(held, "wide", 1)
        out = lax.dynamic_update_slice(out, held[None], (there * 2 + side, 0, 0))
        out = lax.dynamic_update_slice(out, other[None], (there * 2 + 1 - side, 0, 0))
        held = follow
    return out


def scatter_blocks(blocks):
    if not stepwise():
        return lax.psum_scatter(blocks, "wide", scatter_dimension=0, tiled=False).astype(F32)
    count = lax.axis_size("wide")
    lines = count // 2
    me = lax.axis_index("wide")
    line, side = me // 2, me % 2

    def pick(index):
        return lax.dynamic_index_in_dim(blocks, index, 0, keepdims=False)

    total = None
    for k in [*range(1, lines), 0]:
        there = (line - k) % lines
        other = swap(pick(there * 2 + 1 - side), "wide", 1)
        mine = pick(there * 2 + side).astype(F32) + other.astype(F32)
        if total is not None:
            mine = mine + ring(total).astype(F32)
        total = mine.astype(BF16)
    return mine


def on_device(
    states,
    segment_ids,
    attn_gain,
    w_query,
    w_key,
    w_value,
    w_attn_out,
    bias_table,
    mlp_gain,
    w_in_gate,
    w_in_up,
    w_mlp_out,
    gate_gain,
    gate_weight,
    out_cot,
    gate_cot,
):
    wide_count = lax.axis_size("wide")
    block, part = w_query.shape
    hidden = w_in_gate.shape[1]
    width = states.shape[2]
    length = states.shape[1]
    heads = bias_table.shape[1]
    buckets_count = bias_table.shape[0]
    inputs = states[0].astype(F32)
    segments = segment_ids[0]

    vectors = jnp.stack([attn_gain, mlp_gain, gate_gain, gate_weight])
    attn_block = jnp.concatenate([w_query, w_key, w_value, w_attn_out.T], axis=1)
    extra = max(0, block - 4 * part)
    attn_block = jnp.pad(attn_block, ((0, 0), (0, extra)))
    vectors = jnp.pad(vectors, ((0, 4), (0, 4 * part + extra - block)))
    attn_all = gather_blocks(jnp.concatenate([attn_block, vectors], axis=0))
    mats = attn_all[:, :block, : 4 * part].reshape(width, 4 * part)
    full_qkv, full_attn_out = mats[:, : 3 * part], mats[:, 3 * part :]
    vectors = attn_all[:, block : block + 4, :block].transpose(1, 0, 2).reshape(4, width).astype(F32)
    gain_one, gain_two, gain_three, gate_vector = (vectors[i] for i in range(4))
    full_gate = gather_blocks(w_in_gate).reshape(width, hidden)
    full_up = gather_blocks(w_in_up).reshape(width, hidden)
    full_out = gather_blocks(w_mlp_out.T).reshape(width, hidden)

    states_all = gather_rows(states[0]).astype(F32)
    h1_all = (states_all * inverse_rms(states_all) * gain_one).astype(BF16)
    count = lax.axis_size("narrow")
    qkv = product(h1_all, full_qkv).astype(BF16)
    qkv = to_features([qkv[k * length : (k + 1) * length] for k in range(count)])

    def of_heads(which):
        mine = qkv[:, :, which * part : (which + 1) * part]
        return mine.transpose(1, 0, 2).reshape(length, heads, -1)

    def features_of(mine):
        return mine.reshape(length, count, part).transpose(1, 0, 2)

    query, key, value = of_heads(0), of_heads(1), of_heads(2)
    onehot = (
        relative_buckets(length)[:, :, None] == jnp.arange(buckets_count, dtype=jnp.int32)
    ).astype(BF16)
    bias = jnp.einsum("qkb,bh->hqk", onehot, bias_table, preferred_element_type=F32)
    same = (segments[:, None] == segments[None, :])[None]
    scores = jnp.einsum("qhd,khd->hqk", query, key, preferred_element_type=F32) + bias
    scores = jnp.where(same, scores, NEGATIVE)
    expo = jnp.exp(scores - jnp.max(scores, axis=-1, keepdims=True))
    full_probs = expo / jnp.sum(expo, axis=-1, keepdims=True)
    probs = full_probs.astype(BF16)
    attended = jnp.einsum("hqk,khd->qhd", probs, value, preferred_element_type=F32)
    attended = attended.astype(BF16).reshape(length, -1)
    attended_all = to_rows(features_of(attended))
    x2 = inputs + scatter_rows(times_back(attended_all, full_attn_out))

    h2 = (x2 * inverse_rms(x2) * gain_two).astype(BF16)
    h2_all = gather_rows(h2)
    gate_part = product(h2_all, full_gate)
    up_part = product(h2_all, full_up)
    act = gelu_mix(gate_part, up_part).astype(BF16)
    x3 = x2 + scatter_rows(times_back(act, full_out))

    h3 = x3 * inverse_rms(x3) * gain_three
    sig = jax.nn.sigmoid(jnp.sum(h3 * gate_vector, axis=-1))
    gates = -30.0 * sig
    dlogit = gate_cot[0] * -30.0 * sig * (1.0 - sig)
    d_gate_weight = jnp.sum(dlogit[:, None] * h3, axis=0)
    dx3, d_gain_three = norm_back(x3, gain_three, dlogit[:, None] * gate_vector)
    dx3 = dx3 + out_cot[0].astype(F32)

    def summed(left, right):
        grads = outer_sum(left, right).astype(BF16)
        return scatter_blocks(grads.reshape(wide_count, block, -1))

    dm_all = gather_rows(dx3.astype(BF16))
    d_out = summed(dm_all, act)
    dact = product(dm_all, full_out)
    _, pullback = jax.vjp(gelu_mix, gate_part, up_part)
    d_gate_part, d_up_part = pullback(dact)
    d_gate_part = d_gate_part.astype(BF16)
    d_up_part = d_up_part.astype(BF16)
    d_in_gate = summed(h2_all, d_gate_part)
    d_in_up = summed(h2_all, d_up_part)
    dh2 = scatter_rows(times_back(d_gate_part, full_gate) + times_back(d_up_part, full_up))
    dx2, d_gain_two = norm_back(x2, gain_two, dh2)
    dx2 = dx2 + dx3

    da_all = gather_rows(dx2.astype(BF16))
    dout = product(da_all, full_attn_out).astype(BF16)
    dout = to_features([dout[k * length : (k + 1) * length] for k in range(count)])
    dout = dout.transpose(1, 0, 2).reshape(length, heads, -1)
    dprobs = jnp.einsum("qhd,khd->hqk", dout, value, preferred_element_type=F32)
    dscores = full_probs * (dprobs - jnp.sum(dprobs * full_probs, axis=-1, keepdims=True))
    dscores = dscores.astype(BF16)
    d_table = jnp.einsum("qkb,hqk->bh", onehot, dscores, preferred_element_type=F32)
    dquery = jnp.einsum("hqk,khd->qhd", dscores, key, preferred_element_type=F32)
    dkey = jnp.einsum("hqk,qhd->khd", dscores, query, preferred_element_type=F32)
    dvalue = jnp.einsum("hqk,qhd->khd", probs, dout, preferred_element_type=F32)
    dqkv = jnp.concatenate([features_of(a.astype(BF16)) for a in (dquery, dkey, dvalue)], axis=2)
    dqkv = to_rows(dqkv)
    d_attn = jnp.concatenate([outer_sum(h1_all, dqkv), outer_sum(da_all, attended_all)], axis=1)
    d_attn = scatter_blocks(d_attn.astype(BF16).reshape(wide_count, block, 4 * part))
    dh1 = scatter_rows(times_back(dqkv, full_qkv))
    dx1, d_gain_one = norm_back(inputs, gain_one, dh1)
    grad_inputs = (dx1 + dx2).astype(BF16)

    table = jnp.pad(d_table.reshape(-1), (0, width - d_table.size))
    small = jnp.stack([d_gain_one, d_gain_two, d_gain_three, d_gate_weight, table])
    small = total_sum(total_sum(small, "narrow"), "wide")
    mine = lax.dynamic_slice(small, (0, lax.axis_index("wide") * block), (4, block))
    table = small[4, : d_table.size].reshape(d_table.shape)
    return (
        x3.astype(BF16)[None],
        gates[None],
        grad_inputs[None],
        mine[0],
        d_attn[:, :part],
        d_attn[:, part : 2 * part],
        d_attn[:, 2 * part : 3 * part],
        d_attn[:, 3 * part :].T,
        table,
        mine[1],
        d_in_gate,
        d_in_up,
        d_out.T,
        mine[2],
        mine[3],
    )


def solution(mesh):
    in_specs = (
        P(("wide", "narrow"), None, None),
        P(("wide", "narrow"), None),
        P("wide"),
        P("wide", "narrow"),
        P("wide", "narrow"),
        P("wide", "narrow"),
        P("narrow", "wide"),
        P(),
        P("wide"),
        P("wide", "narrow"),
        P("wide", "narrow"),
        P("narrow", "wide"),
        P("wide"),
        P("wide"),
        P(("wide", "narrow"), None, None),
        P(("wide", "narrow"), None),
    )
    out_specs = (
        P(("wide", "narrow"), None, None),
        P(("wide", "narrow"), None),
        P(("wide", "narrow"), None, None),
        P("wide"),
        P("wide", "narrow"),
        P("wide", "narrow"),
        P("wide", "narrow"),
        P("narrow", "wide"),
        P(),
        P("wide"),
        P("wide", "narrow"),
        P("wide", "narrow"),
        P("narrow", "wide"),
        P("wide"),
        P("wide"),
    )
    return jax.shard_map(
        on_device, mesh=mesh, in_specs=in_specs, out_specs=out_specs, check_vma=False
    )
```
